512 devices in a mesh: ctx: 128 (over x, y_lo, z, core), rec: 4 (over y_hi).
Axes of the slice: x: 4, y: 8 (y_hi: 4, y_lo: 2; y = y_hi * 2 + y_lo), z: 8, core: 2. Of those that a mesh axis runs over, the one named last changes fastest.
Arguments:
- queries: bfloat16 [4, 16384, 4096], P('rec', 'ctx'), may hold values from -6 to 6
- out_grads: bfloat16 [4, 16384, 4096], P('rec', 'ctx'), may hold values from -6 to 6
- log_sums: float32 [4, 32, 16384], P('rec', None, 'ctx'), may hold values from 1.5 to 4
- deltas: float32 [4, 32, 16384], P('rec', None, 'ctx'), may hold values from -6 to 6
- keys: bfloat16 [16384, 256], P('ctx'), may hold values from -6 to 6
- values: bfloat16 [16384, 256], P('ctx'), may hold values from -0.5 to 0.5
- doc_ids: int32 [4, 128], P('rec'), may hold values from 0 to 63, never falling along the last dimension, each value on 1 to 4 neighbouring positions
Outputs:
- query_grads: bfloat16 [4, 16384, 4096], P('rec', 'ctx')
- key_grads: bfloat16 [16384, 256], P(('ctx', 'rec'))
- value_grads: bfloat16 [16384, 256], P(('ctx', 'rec'))
The draws below stay inside these ranges and needn't reach their ends.
Inputs may be any that keep to these rules, and one draw needn't show every extreme that they name: `doc_ids`: in each row the numbers never fall, start at 0, each document spans 1 to 4 blocks and some document spans exactly 4 blocks.
All inputs are finite; a program needn't handle non-finite values.
Results may differ from the reference program's by a relative error of at most 0.0062.
Values may be sent and summed in bfloat16 or wider, within the bound.
No kernel may reach another device: no remote copies, remote signals or barrier semaphores. Data moves between devices by JAX's collectives and lax.ppermute only.
A program may use at most 64 MiB of HBM per device.

```python
import math
import jax
import jax.numpy as jnp
import numpy as np
from jax import lax

QH = 32
KVH = 2
HD = 128
TOK = 128
MAXSPAN = 4
NBLK = 128
REC = 4
TOKENS = 16384


def block_scale(key, dims, pieces, low, top_value):
    factor_of, own = 1.0, jax.random.fold_in(key, 6)
    for position, shards_of in pieces:
        heights = jnp.exp(jax.random.uniform(jax.random.fold_in(own, position), (shards_of,), jnp.float32, low / len(pieces), top_value / len(pieces)))
        factor_of = factor_of * jnp.repeat(heights, dims[position] // shards_of).reshape([-1 if axis == position else 1 for axis in range(len(dims))])
    return factor_of


def split_up(amount, total, limit, skew):
    loads = [(1 << 20) // math.isqrt(rank ** skew) + 1 for rank in range(2, amount + 1)]
    spare, holding = total - limit - (amount - 1), [1] * (amount - 1)
    while spare > 0:
        free = [i for i in range(amount - 1) if holding[i] < limit]
        pool, budget = sum([loads[i] for i in free]), spare
        for i in free:
            addition = min(limit - holding[i], max(1, budget * loads[i] // pool), spare)
            holding[i] = holding[i] + addition
            spare = spare - addition
    return np.array([limit] + holding)


def ragged_sizes(stream_key, count, total, bound, slope):
    if count == 2:
        one = jax.random.randint(stream_key, (), max(1, total - bound), min(bound, total - 1) + 1)
        return jnp.stack([one, total - one])
    lengths = jnp.asarray(split_up(count, total, bound, slope), jnp.int32)
    couples = (count - 1) // 2
    donor, taker = lengths[1:1 + 2 * couples:2], lengths[2:2 + 2 * couples:2]
    slack = jnp.minimum(donor - 1, bound - taker)
    shifted = jax.random.randint(jax.random.fold_in(stream_key, 1), (couples,), 0, 1 << 20) % (slack + 1)
    lengths = lengths.at[1:1 + 2 * couples:2].set(donor - shifted).at[2:2 + 2 * couples:2].set(taker + shifted)
    return lengths[jax.random.permutation(jax.random.fold_in(stream_key, 2), count)]


def normal_values(key, extent, scale, most, pieces=(), kind=jnp.bfloat16):
    result = jax.random.normal(key, extent, jnp.float32) * scale
    if len(pieces) > 0:
        result = block_scale(key, extent, pieces, -0.22, 0.18) * result
    return jnp.clip(result, min=-most, max=most).astype(kind)


def setup_inputs(seed: int = 0) -> dict:
    arg_keys = jax.random.split(jax.random.key(seed), 8)
    queries = normal_values(arg_keys[0], (REC, TOKENS, QH * HD), 1.0, 6.0, ((0, 4), (1, 128)))
    out_grads = normal_values(arg_keys[1], (REC, TOKENS, QH * HD), 1.0, 6.0, ((0, 4), (1, 128)))
    log_sums = jnp.clip(1.5 + 2.5 * jax.random.uniform(arg_keys[2], (REC, QH, TOKENS), jnp.float32) ** block_scale(arg_keys[2], (REC, QH, TOKENS), ((0, 4), (2, 128)), -0.2, 0.2), 1.5, 4.0)
    deltas = normal_values(arg_keys[3], (REC, QH, TOKENS), 1.0, 6.0, ((0, 4), (2, 128)), jnp.float32)
    keys = normal_values(arg_keys[4], (TOKENS, KVH * HD), 1.0, 6.0, ((0, 128),))
    values = normal_values(arg_keys[5], (TOKENS, KVH * HD), HD ** -0.5, 0.5, ((0, 128),))
    doc_ids = jax.vmap(lambda own: jnp.searchsorted(jnp.cumsum(ragged_sizes(own, NBLK // 2, NBLK, MAXSPAN, 1)), jnp.arange(NBLK), side="right"))(jax.random.split(arg_keys[6], REC)).reshape((REC, NBLK)).astype(jnp.int32)
    return {"queries": queries, "out_grads": out_grads, "log_sums": log_sums, "deltas": deltas, "keys": keys, "values": values, "doc_ids": doc_ids}


def tile_terms(query_block, grad_block, sums_block, delta_block, key_block, value_block, query_index, key_index):
    rows = query_block.shape[0]
    key_heads = key_block.shape[1] // HD
    group = query_block.shape[1] // (key_heads * HD)
    scale = HD ** -0.5
    query_heads = query_block.astype(jnp.float32).reshape(rows, key_heads, group, HD)
    grad_heads = grad_block.astype(jnp.float32).reshape(rows, key_heads, group, HD)
    key_split = key_block.astype(jnp.float32).reshape(rows, key_heads, HD)
    value_split = value_block.astype(jnp.float32).reshape(rows, key_heads, HD)
    sums_heads = sums_block.reshape(key_heads, group, rows)
    delta_heads = delta_block.reshape(key_heads, group, rows)
    positions = jnp.arange(rows, dtype=jnp.int32)
    query_pos = query_index * rows + positions
    key_pos = key_index * rows + positions
    causal = key_pos[None, :] <= query_pos[:, None]
    scores = jnp.einsum("qkgd,skd->kgqs", query_heads, key_split) * scale
    probs = jnp.where(causal, jnp.exp(scores - sums_heads[..., None]), 0.0)
    dprobs = jnp.einsum("qkgd,skd->kgqs", grad_heads, value_split)
    dscores = probs * (dprobs - delta_heads[..., None])
    probs_b = probs.astype(jnp.bfloat16).astype(jnp.float32)
    dscores_b = dscores.astype(jnp.bfloat16).astype(jnp.float32)
    value_grad = jnp.einsum("kgqs,qkgd->skd", probs_b, grad_heads).reshape(rows, key_heads * HD)
    key_grad = jnp.einsum("kgqs,qkgd->skd", dscores_b, query_heads).reshape(rows, key_heads * HD) * scale
    query_grad = jnp.einsum("kgqs,skd->qkgd", dscores_b, key_split).reshape(rows, -1) * scale
    return query_grad, key_grad, value_grad


def reference(queries, out_grads, log_sums, deltas, keys, values, doc_ids):
    rows = TOK
    span = MAXSPAN
    blocks = NBLK
    width = keys.shape[1]
    qwidth = queries.shape[2]
    pad_rows = (span - 1) * rows
    keys_pad = jnp.concatenate([jnp.zeros((pad_rows, width), keys.dtype), keys], axis=0)
    values_pad = jnp.concatenate([jnp.zeros((pad_rows, width), values.dtype), values], axis=0)
    key_total = jnp.zeros((pad_rows + TOKENS, width), jnp.float32)
    value_total = jnp.zeros((pad_rows + TOKENS, width), jnp.float32)
    order = jnp.arange(blocks, dtype=jnp.int32)
    results = []
    for recur in range(REC):
        ids = doc_ids[recur]
        first = jnp.min(jnp.where(ids[:, None] == ids[None, :], order[None, :], blocks), axis=1).astype(jnp.int32)
        query_all = queries[recur]
        grad_all = out_grads[recur]
        sums_all = log_sums[recur]
        delta_all = deltas[recur]

        def per_block(carry, index):
            key_acc, value_acc = carry
            start = (index * rows).astype(jnp.int32)
            query_block = lax.dynamic_slice_in_dim(query_all, start, rows, 0)
            grad_block = lax.dynamic_slice_in_dim(grad_all, start, rows, 0)
            sums_block = lax.dynamic_slice_in_dim(sums_all, start, rows, 1)
            delta_block = lax.dynamic_slice_in_dim(delta_all, start, rows, 1)
            query_grad = jnp.zeros((rows, qwidth), jnp.float32)
            for back in range(span):
                other = index - back
                kstart = ((other + span - 1) * rows).astype(jnp.int32)
                key_block = lax.dynamic_slice_in_dim(keys_pad, kstart, rows, 0)
                value_block = lax.dynamic_slice_in_dim(values_pad, kstart, rows, 0)
                active = other >= first[index]

                def compute():
                    return tile_terms(query_block, grad_block, sums_block, delta_block, key_block, value_block, index, other)

                def nothing():
                    return (jnp.zeros((rows, qwidth), jnp.float32), jnp.zeros((rows, width), jnp.float32), jnp.zeros((rows, width), jnp.float32))

                terms = lax.cond(active, compute, nothing)
                query_grad = query_grad + terms[0]
                key_acc = lax.dynamic_update_slice_in_dim(key_acc, lax.dynamic_slice_in_dim(key_acc, kstart, rows, 0) + terms[1], kstart, 0)
                value_acc = lax.dynamic_update_slice_in_dim(value_acc, lax.dynamic_slice_in_dim(value_acc, kstart, rows, 0) + terms[2], kstart, 0)
            return (key_acc, value_acc), query_grad.astype(jnp.bfloat16)

        (key_total, value_total), grads = lax.scan(per_block, (key_total, value_total), order)
        results.append(grads.reshape(TOKENS, qwidth))
    query_grads = jnp.stack(results, axis=0)
    return query_grads, key_total[pad_rows:].astype(jnp.bfloat16), value_total[pad_rows:].astype(jnp.bfloat16)
```

```python
import math

import jax
import jax.numpy as jnp
from jax import lax
from jax.experimental import pallas as pl
from jax.experimental.pallas import tpu as pltpu
from jax.sharding import PartitionSpec as P

HD = 128
TOK = 128
SPAN = 4
HEADS = 32
GROUP = 16
TOGETHER = 4
SCALE = HD**-0.5
LOG2E = math.log2(math.e)
FAR = 1e30


def dot_nt(a, b):
    return lax.dot_general(a, b, (((1,), (1,)), ((), ())), preferred_element_type=jnp.float32)


def dot_nn(a, b):
    return lax.dot_general(a, b, (((1,), (0,)), ((), ())), preferred_element_type=jnp.float32)


def attention_kernel(
    ids, q_ref, o_ref, lse_ref, delta_ref, k_ref, v_ref, r1, r2, r3,
    dq_ref, keep_ref, send_ref, ks, vs, kts, dk, dv,
):
    me = lax.axis_index("ctx")
    away = [jnp.float32(0.0)]
    for back in range(1, SPAN):
        at = jnp.maximum(me - back, 0)
        live = jnp.logical_and(me >= back, ids[0, at] == ids[0, me])
        away.append(jnp.where(live, jnp.float32(0.0), jnp.float32(FAR)))
    for g in range(2):
        cols = slice(g * HD, (g + 1) * HD)
        later = slice((g + 2) * HD, (g + 3) * HD)
        for back in range(SPAN):
            at = slice(back * TOK, (back + 1) * TOK)
            got = (None, r1, r2, r3)[back]
            kb = k_ref[:, cols] if back == 0 else got[:, cols]
            vb = v_ref[:, cols] if back == 0 else got[:, later]
            ks[g, at, :] = kb
            vs[g, at, :] = vb
            kts[g, :, at] = kb.T
    dk[...] = jnp.zeros_like(dk)
    dv[...] = jnp.zeros_like(dv)
    key_at = lax.broadcasted_iota(jnp.int32, (TOK, TOK), 0)
    causal = key_at <= lax.broadcasted_iota(jnp.int32, (TOK, TOK), 1)
    for g in range(2):

        def step(i, carry):
            head = g * GROUP + i * TOGETHER
            col = pl.multiple_of(head * HD, TOGETHER * HD)
            qs = q_ref[:, pl.ds(col, TOGETHER * HD)]
            os = o_ref[:, pl.ds(col, TOGETHER * HD)]
            q = jnp.concatenate([qs[:, j * HD : (j + 1) * HD] for j in range(TOGETHER)], 0)
            o = jnp.concatenate([os[:, j * HD : (j + 1) * HD] for j in range(TOGETHER)], 0)
            scores = dot_nt(ks[g], q)
            dprobs = dot_nt(vs[g], o)
            probs_b, dscores_b = [], []
            for j in range(TOGETHER):
                sums = lse_ref[pl.ds(head + j, 1), :] * LOG2E
                delta = delta_ref[pl.ds(head + j, 1), :]
                p_rows, d_rows = [], []
                for back in range(SPAN):
                    tile = (
                        slice(back * TOK, (back + 1) * TOK),
                        slice(j * TOK, (j + 1) * TOK),
                    )
                    p = jnp.exp2(scores[tile] * (SCALE * LOG2E) - (sums + away[back]))
                    if back == 0:
                        p = jnp.where(causal, p, 0.0)
                    p_rows.append(p.astype(jnp.bfloat16))
                    d_rows.append((p * (dprobs[tile] - delta)).astype(jnp.bfloat16))
                probs_b.append(jnp.concatenate(p_rows, 0))
                dscores_b.append(jnp.concatenate(d_rows, 0))
            probs_b = jnp.concatenate(probs_b, 1)
            dscores_b = jnp.concatenate(dscores_b, 1)
            dv[g] += dot_nn(probs_b, o)
            dk[g] += dot_nn(dscores_b, q)
            dqt = (dot_nn(kts[g], dscores_b) * SCALE).astype(jnp.bfloat16)
            for j in range(TOGETHER):
                at = pl.multiple_of(col + j * HD, HD)
                dq_ref[:, pl.ds(at, HD)] = dqt[:, j * TOK : (j + 1) * TOK].T
            return carry

        lax.fori_loop(0, GROUP // TOGETHER, step, 0)
    for g in range(2):
        cols = slice(g * HD, (g + 1) * HD)
        later = slice((g + 2) * HD, (g + 3) * HD)
        for back in range(SPAN):
            at = slice(back * TOK, (back + 1) * TOK)
            key_part = dk[g, at, :] * SCALE
            value_part = dv[g, at, :]
            if back == 0:
                keep_ref[:, cols] = key_part
                keep_ref[:, later] = value_part
            else:
                send_ref[back - 1, :, cols] = key_part.astype(jnp.bfloat16)
                send_ref[back - 1, :, later] = value_part.astype(jnp.bfloat16)


def attention(ids, q, o, lse, delta, k, v, r1, r2, r3):
    vmem = pl.BlockSpec(memory_space=pltpu.VMEM)
    width = 4 * HD
    return pl.pallas_call(
        attention_kernel,
        out_shape=(
            jax.ShapeDtypeStruct(q.shape, jnp.bfloat16),
            jax.ShapeDtypeStruct((TOK, width), jnp.float32),
            jax.ShapeDtypeStruct((SPAN - 1, TOK, width), jnp.bfloat16),
        ),
        in_specs=[pl.BlockSpec(memory_space=pltpu.SMEM)] + [vmem] * 9,
        out_specs=(vmem, vmem, vmem),
        scratch_shapes=[
            pltpu.VMEM((2, SPAN * TOK, HD), jnp.bfloat16),
            pltpu.VMEM((2, SPAN * TOK, HD), jnp.bfloat16),
            pltpu.VMEM((2, HD, SPAN * TOK), jnp.bfloat16),
            pltpu.VMEM((2, SPAN * TOK, HD), jnp.float32),
            pltpu.VMEM((2, SPAN * TOK, HD), jnp.float32),
        ],
        compiler_params=pltpu.CompilerParams(vmem_limit_bytes=24 << 20),
        cost_estimate=pl.CostEstimate(
            flops=10 * HEADS * SPAN * TOK * TOK * HD,
            bytes_accessed=5 << 20,
            transcendentals=HEADS * SPAN * TOK * TOK,
        ),
    )(ids, q, o, lse, delta, k, v, r1, r2, r3)


def shifted(block, by):
    devices = range(lax.axis_size("ctx"))
    return lax.ppermute(block, "ctx", [(i, i + by) for i in devices if i + by in devices])


def per_device(queries, out_grads, log_sums, deltas, keys, values, doc_ids):
    both = jnp.concatenate([keys, values], axis=1)
    behind = [shifted(both, by) for by in range(1, SPAN)]
    query_grad, total, parts = attention(
        doc_ids, queries[0], out_grads[0], log_sums[0], deltas[0], keys, values, *behind
    )
    for by in range(1, SPAN):
        total = total + shifted(parts[by - 1], -by).astype(jnp.float32)
    peers = lax.axis_size("rec")
    pieces = total.astype(jnp.bfloat16).reshape(peers, TOK // peers, -1)
    arrived = lax.all_to_all(pieces, "rec", 0, 0, tiled=True)
    summed = arrived.astype(jnp.float32).sum(axis=0).astype(jnp.bfloat16)
    return query_grad[None], summed[:, : 2 * HD], summed[:, 2 * HD :]


def solution(mesh):
    return jax.shard_map(
        per_device,
        mesh=mesh,
        in_specs=(
            P("rec", "ctx", None),
            P("rec", "ctx", None),
            P("rec", None, "ctx"),
            P("rec", None, "ctx"),
            P("ctx", None),
            P("ctx", None),
            P("rec", None),
        ),
        out_specs=(P("rec", "ctx", None), P(("ctx", "rec"), None), P(("ctx", "rec"), None)),
        check_vma=False,
    )
```

```python
import functools
import math

import jax
import jax.numpy as jnp
from jax import lax
from jax.experimental import pallas as pl
from jax.experimental.pallas import tpu as pltpu
from jax.sharding import PartitionSpec as P

HD = 128
TOK = 128
SPAN = 4
HEADS = 32
GROUP = 16
CHUNK = 2
WIDTH = HEADS * HD
HALF = GROUP * HD
SCALE = HD**-0.5
LOG2E = math.log2(math.e)
FAR = 1e30
BF16 = jnp.bfloat16
F32 = jnp.float32
EARLY, LATE = (1, 2), (3,)

VMEM = pl.BlockSpec(memory_space=pltpu.VMEM)
HBM = pl.BlockSpec(memory_space=pltpu.HBM)
SMEM = pl.BlockSpec(memory_space=pltpu.SMEM)
SHAPE = jax.ShapeDtypeStruct
PART = SHAPE((TOK, 4 * HD), BF16)


def in_hbm(*arrays):
    return [pltpu.with_memory_space_constraint(a, pltpu.HBM) for a in arrays]


def in_vmem(*arrays):
    return [pltpu.with_memory_space_constraint(a, pltpu.VMEM) for a in arrays]


def settings(name, blocks, dots):
    return dict(
        name=name,
        compiler_params=pltpu.CompilerParams(vmem_limit_bytes=16 << 20),
        cost_estimate=pl.CostEstimate(
            flops=2 * dots * blocks * HEADS * TOK * TOK * HD,
            bytes_accessed=2 << 20,
            transcendentals=blocks * HEADS * TOK * TOK,
        ),
    )


def dot_nt(a, b):
    return lax.dot_general(a, b, (((1,), (1,)), ((), ())), preferred_element_type=F32)


def dot_nn(a, b):
    return lax.dot_general(a, b, (((1,), (0,)), ((), ())), preferred_element_type=F32)


def join_kernel(k, v, both, sem):
    copies = [
        pltpu.make_async_copy(k, both.at[:, : 2 * HD], sem.at[0]),
        pltpu.make_async_copy(v, both.at[:, 2 * HD :], sem.at[1]),
    ]
    for c in copies:
        c.start()
    for c in copies:
        c.wait()


def join(k, v):
    return pl.pallas_call(
        join_kernel,
        out_shape=PART,
        in_specs=[HBM, HBM],
        out_specs=VMEM,
        scratch_shapes=[pltpu.SemaphoreType.DMA((2,))],
        name="join",
    )(*in_hbm(k, v))


def head_rows(ref, head, count):
    return jnp.concatenate([ref[:, h * HD : (h + 1) * HD] for h in range(head, head + count)], 0)


def grad_tiles(g, both, away, causal, q_ref, o_ref, sums_ref, delta_ref, dscores, parts, probs):
    blocks = len(both)
    k = jnp.concatenate([b[:, g * HD : (g + 1) * HD] for b in both], 0)
    v = jnp.concatenate([b[:, (g + 2) * HD : (g + 3) * HD] for b in both], 0)

    def products(i):
        head = g * GROUP + i * CHUNK
        return dot_nt(k, head_rows(q_ref, head, CHUNK)), dot_nt(v, head_rows(o_ref, head, CHUNK))

    ahead = products(0)
    for i in range(GROUP // CHUNK):
        scores, dprobs = ahead
        if (i + 1) * CHUNK < GROUP:
            ahead = products(i + 1)
        p_cols, d_cols = [], []
        for j in range(CHUNK):
            head = g * GROUP + i * CHUNK + j
            sums = sums_ref[head : head + 1, :] * LOG2E
            delta = delta_ref[head : head + 1, :]
            p_rows, d_rows = [], []
            for b in range(blocks):
                tile = slice(b * TOK, (b + 1) * TOK), slice(j * TOK, (j + 1) * TOK)
                less = sums if away is None else sums + away[b]
                p = jnp.exp2(scores[tile] * (SCALE * LOG2E) - less)
                if causal is not None:
                    p = jnp.where(causal, p, 0.0)
                p_rows.append(p.astype(BF16))
                d_rows.append((p * (dprobs[tile] - delta)).astype(BF16))
            p_cols.append(jnp.concatenate(p_rows, 0))
            d_cols.append(jnp.concatenate(d_rows, 0))
        at = i * CHUNK * TOK
        probs[:, at : at + CHUNK * TOK] = jnp.concatenate(p_cols, 1)
        at += g * HALF
        dscores[:, at : at + CHUNK * TOK] = jnp.concatenate(d_cols, 1)
    value_grad = dot_nn(probs[...], head_rows(o_ref, g * GROUP, GROUP))
    key_grad = dot_nn(dscores[:, g * HALF : (g + 1) * HALF], head_rows(q_ref, g * GROUP, GROUP))
    for b, part in enumerate(parts):
        rows = slice(b * TOK, (b + 1) * TOK)
        part[:, g * HD : (g + 1) * HD] = (key_grad[rows] * SCALE).astype(part.dtype)
        part[:, (g + 2) * HD : (g + 3) * HD] = value_grad[rows].astype(part.dtype)


def distances(ids, blocks):
    me = lax.axis_index("ctx")
    away = []
    for back in blocks:
        at = jnp.maximum(me - back, 0)
        live = jnp.logical_and(me >= back, ids[0, at] == ids[0, me])
        away.append(jnp.where(live, F32(0.0), F32(FAR)))
    return away


def early_kernel(blocks, ids_hbm, q_hbm, o_hbm, sums_hbm, delta_hbm, *refs):
    n = len(blocks)
    both, refs = refs[:n], refs[n:]
    q, o, sums, delta, dscores = refs[:5]
    parts, (ids, probs, sem) = refs[5 : 5 + n], refs[5 + n :]
    small = [
        pltpu.make_async_copy(ids_hbm, ids, sem.at[0]),
        pltpu.make_async_copy(sums_hbm, sums, sem.at[1]),
        pltpu.make_async_copy(delta_hbm, delta, sem.at[2]),
    ]
    halves = []
    for g in range(2):
        cols = pl.ds(g * HALF, HALF)
        halves.append(
            [
                pltpu.make_async_copy(q_hbm.at[:, cols], q.at[:, cols], sem.at[3 + 2 * g]),
                pltpu.make_async_copy(o_hbm.at[:, cols], o.at[:, cols], sem.at[4 + 2 * g]),
            ]
        )
    for c in small + halves[0] + halves[1]:
        c.start()
    for c in small:
        c.wait()
    away = distances(ids, blocks)
    for g in range(2):
        for c in halves[g]:
            c.wait()
        grad_tiles(g, both, away, None, q, o, sums, delta, dscores, parts, probs)


def early(ids, q, o, sums, delta, both):
    n = len(both)
    return pl.pallas_call(
        functools.partial(early_kernel, EARLY),
        out_shape=[
            SHAPE(q.shape, BF16),
            SHAPE(o.shape, BF16),
            SHAPE(sums.shape, F32),
            SHAPE(delta.shape, F32),
            SHAPE((n * TOK, WIDTH), BF16),
        ]
        + [PART] * n,
        in_specs=[HBM] * 5 + [VMEM] * n,
        out_specs=[VMEM] * (5 + n),
        scratch_shapes=[
            pltpu.SMEM(ids.shape, jnp.int32),
            pltpu.VMEM((n * TOK, HALF), BF16),
            pltpu.SemaphoreType.DMA((7,)),
        ],
        **settings("early", n, 4),
    )(*in_hbm(ids, q, o, sums, delta), *both)


def late_kernel(blocks, ids, q, o, sums, delta, *refs):
    n = len(blocks)
    both, dscores, parts, probs = refs[:n], refs[n], refs[n + 1 : -1], refs[-1]
    away = distances(ids, blocks)
    for g in range(2):
        grad_tiles(g, both, away, None, q, o, sums, delta, dscores, parts, probs)


def late(ids, q, o, sums, delta, both):
    n = len(both)
    return pl.pallas_call(
        functools.partial(late_kernel, LATE),
        out_shape=[SHAPE((n * TOK, WIDTH), BF16)] + [PART] * n,
        in_specs=[SMEM] + [VMEM] * (4 + n),
        out_specs=[VMEM] * (1 + n),
        scratch_shapes=[pltpu.VMEM((n * TOK, HALF), BF16)],
        **settings("late", n, 4),
    )(ids, q, o, sums, delta, *both)


def own_kernel(q, o, sums, delta, *refs):
    both, dscores = refs[:SPAN], refs[SPAN : SPAN + 2]
    dq_hbm, part, dq, own, probs, sem = refs[SPAN + 2 :]
    key_at = lax.broadcasted_iota(jnp.int32, (TOK, TOK), 0)
    causal = key_at <= lax.broadcasted_iota(jnp.int32, (TOK, TOK), 1)
    copies = []
    for g in range(2):
        grad_tiles(g, both[:1], None, causal, q, o, sums, delta, own, (part,), probs)
        cols = slice(g * HALF, (g + 1) * HALF)
        kt = jnp.concatenate([b[:, g * HD : (g + 1) * HD].T for b in both], 1)
        d = jnp.concatenate([r[:, cols] for r in (own, *dscores)], 0)
        dqt = (dot_nn(kt, d) * SCALE).astype(BF16)
        for j in range(GROUP):
            at = g * HALF + j * HD
            dq[:, at : at + HD] = dqt[:, j * TOK : (j + 1) * TOK].T
        copies.append(pltpu.make_async_copy(dq.at[:, cols], dq_hbm.at[:, cols], sem.at[g]))
        copies[-1].start()
    for c in copies:
        c.wait()


def own(q, o, sums, delta, both, dscores):
    return pl.pallas_call(
        own_kernel,
        out_shape=[SHAPE(q.shape, BF16), SHAPE((TOK, 4 * HD), F32)],
        in_specs=[VMEM] * (4 + SPAN + 2),
        out_specs=[HBM, VMEM],
        scratch_shapes=[
            pltpu.VMEM((TOK, WIDTH), BF16),
            pltpu.VMEM((TOK, WIDTH), BF16),
            pltpu.VMEM((TOK, HALF), BF16),
            pltpu.SemaphoreType.DMA((2,)),
        ],
        **settings("own", 2, 4),
    )(*in_vmem(q, o, sums, delta, *both, *dscores))


def shifted(block, by):
    devices = range(lax.axis_size("ctx"))
    return lax.ppermute(block, "ctx", [(i, i + by) for i in devices if i + by in devices])


def per_device(queries, out_grads, log_sums, deltas, keys, values, doc_ids):
    both = [join(keys, values)]
    both += [shifted(both[0], by) for by in range(1, SPAN)]
    q, o, sums, delta, far, *parts = early(
        doc_ids, queries[0], out_grads[0], log_sums[0], deltas[0], [both[b] for b in EARLY]
    )
    farther, *others = late(doc_ids, q, o, sums, delta, [both[b] for b in LATE])
    parts += others
    query_grad, total = own(q, o, sums, delta, both, (far, farther))
    for by in range(1, SPAN):
        total = total + shifted(parts[by - 1], -by).astype(F32)
    peers = lax.axis_size("rec")
    pieces = total.astype(BF16).reshape(peers, TOK // peers, -1)
    arrived = lax.all_to_all(pieces, "rec", 0, 0, tiled=True)
    summed = arrived.astype(F32).sum(axis=0).astype(BF16)
    return query_grad[None], summed[:, : 2 * HD], summed[:, 2 * HD :]


def solution(mesh):
    return jax.shard_map(
        per_device,
        mesh=mesh,
        in_specs=(
            P("rec", "ctx", None),
            P("rec", "ctx", None),
            P("rec", None, "ctx"),
            P("rec", None, "ctx"),
            P("ctx", None),
            P("ctx", None),
            P("rec", None),
        ),
        out_specs=(P("rec", "ctx", None), P(("ctx", "rec"), None), P(("ctx", "rec"), None)),
        check_vma=False,
    )
```

```python
import functools
import math

import jax
import jax.numpy as jnp
from jax import lax
from jax.experimental import pallas as pl
from jax.experimental.pallas import tpu as pltpu
from jax.sharding import PartitionSpec as P

HD = 128
TOK = 128
SPAN = 4
HEADS = 32
GROUP = 16
CHUNK = 2
WIDTH = HEADS * HD
HALF = GROUP * HD
SCALE = HD**-0.5
LOG2E = math.log2(math.e)
FAR = 1e30
BF16 = jnp.bfloat16
F32 = jnp.float32
EARLY, LATE = (3,), (2, 1)

VMEM = pl.BlockSpec(memory_space=pltpu.VMEM)
HBM = pl.BlockSpec(memory_space=pltpu.HBM)
SMEM = pl.BlockSpec(memory_space=pltpu.SMEM)
SHAPE = jax.ShapeDtypeStruct
PART = SHAPE((TOK, 4 * HD), BF16)


def in_hbm(*arrays):
    return [pltpu.with_memory_space_constraint(a, pltpu.HBM) for a in arrays]


def in_vmem(*arrays):
    return [pltpu.with_memory_space_constraint(a, pltpu.VMEM) for a in arrays]


def settings(name, blocks, dots, mib):
    return dict(
        name=name,
        compiler_params=pltpu.CompilerParams(vmem_limit_bytes=mib << 20),
        cost_estimate=pl.CostEstimate(
            flops=2 * dots * blocks * HEADS * TOK * TOK * HD,
            bytes_accessed=2 << 20,
            transcendentals=blocks * HEADS * TOK * TOK,
        ),
    )


def dot_nt(a, b):
    return lax.dot_general(a, b, (((1,), (1,)), ((), ())), preferred_element_type=F32)


def dot_nn(a, b):
    return lax.dot_general(a, b, (((1,), (0,)), ((), ())), preferred_element_type=F32)


def join_kernel(k, v, both, sem):
    copies = [
        pltpu.make_async_copy(k, both.at[:, : 2 * HD], sem.at[0]),
        pltpu.make_async_copy(v, both.at[:, 2 * HD :], sem.at[1]),
    ]
    for c in copies:
        c.start()
    for c in copies:
        c.wait()


def join(k, v):
    return pl.pallas_call(
        join_kernel,
        out_shape=PART,
        in_specs=[HBM, HBM],
        out_specs=VMEM,
        scratch_shapes=[pltpu.SemaphoreType.DMA((2,))],
        **settings("join", 0, 0, 1),
    )(*in_hbm(k, v))


def head_rows(ref, head, count):
    return jnp.concatenate([ref[:, h * HD : (h + 1) * HD] for h in range(head, head + count)], 0)


def grad_tiles(g, both, away, causal, q_ref, o_ref, sums_ref, delta_ref, dscores, parts, probs):
    blocks = len(both)
    k = jnp.concatenate([b[:, g * HD : (g + 1) * HD] for b in both], 0)
    v = jnp.concatenate([b[:, (g + 2) * HD : (g + 3) * HD] for b in both], 0)

    def products(i):
        head = g * GROUP + i * CHUNK
        return dot_nt(k, head_rows(q_ref, head, CHUNK)), dot_nt(v, head_rows(o_ref, head, CHUNK))

    ahead = products(0)
    for i in range(GROUP // CHUNK):
        scores, dprobs = ahead
        if (i + 1) * CHUNK < GROUP:
            ahead = products(i + 1)
        p_cols, d_cols = [], []
        for j in range(CHUNK):
            head = g * GROUP + i * CHUNK + j
            sums = sums_ref[head : head + 1, :] * LOG2E
            delta = delta_ref[head : head + 1, :]
            p_rows, d_rows = [], []
            for b in range(blocks):
                tile = slice(b * TOK, (b + 1) * TOK), slice(j * TOK, (j + 1) * TOK)
                less = sums if away is None else sums + away[b]
                p = jnp.exp2(scores[tile] * (SCALE * LOG2E) - less)
                if causal is not None:
                    p = jnp.where(causal, p, 0.0)
                p_rows.append(p.astype(BF16))
                d_rows.append((p * (dprobs[tile] - delta)).astype(BF16))
            p_cols.append(jnp.concatenate(p_rows, 0))
            d_cols.append(jnp.concatenate(d_rows, 0))
        at = i * CHUNK * TOK
        probs[:, at : at + CHUNK * TOK] = jnp.concatenate(p_cols, 1)
        at += g * HALF
        dscores[:, at : at + CHUNK * TOK] = jnp.concatenate(d_cols, 1)
    value_grad = dot_nn(probs[...], head_rows(o_ref, g * GROUP, GROUP))
    key_grad = dot_nn(dscores[:, g * HALF : (g + 1) * HALF], head_rows(q_ref, g * GROUP, GROUP))
    for b, part in enumerate(parts):
        rows = slice(b * TOK, (b + 1) * TOK)
        part[:, g * HD : (g + 1) * HD] = (key_grad[rows] * SCALE).astype(part.dtype)
        part[:, (g + 2) * HD : (g + 3) * HD] = value_grad[rows].astype(part.dtype)


def distances(ids, blocks):
    me = lax.axis_index("ctx")
    away = []
    for back in blocks:
        at = jnp.maximum(me - back, 0)
        live = jnp.logical_and(me >= back, ids[0, at] == ids[0, me])
        away.append(jnp.where(live, F32(0.0), F32(FAR)))
    return away


def load_kernel(*refs):
    n = len(refs) // 2
    copies = [pltpu.make_async_copy(refs[i], refs[n + i], refs[-1].at[i]) for i in range(n)]
    for c in copies:
        c.start()
    for c in copies:
        c.wait()


def load(*arrays):
    n = len(arrays)
    return pl.pallas_call(
        load_kernel,
        out_shape=[SHAPE(a.shape, a.dtype) for a in arrays],
        in_specs=[HBM] * n,
        out_specs=[VMEM] * n,
        scratch_shapes=[pltpu.SemaphoreType.DMA((n,))],
        **settings("load", 1, 1, 2),
    )(*in_hbm(*arrays))


def behind_kernel(blocks, ids, q, o, sums, delta, *refs):
    n = len(blocks)
    both, dscores, parts, probs = refs[:n], refs[n], refs[n + 1 : -1], refs[-1]
    away = distances(ids, blocks)
    for g in range(2):
        grad_tiles(g, both, away, None, q, o, sums, delta, dscores, parts, probs)


def behind(name, blocks, ids, q, o, sums, delta, both):
    n = len(blocks)
    return pl.pallas_call(
        functools.partial(behind_kernel, blocks),
        out_shape=[SHAPE((n * TOK, WIDTH), BF16)] + [PART] * n,
        in_specs=[SMEM] + [VMEM] * (4 + n),
        out_specs=[VMEM] * (1 + n),
        scratch_shapes=[pltpu.VMEM((n * TOK, HALF), BF16)],
        **settings(name, n, 4, 12),
    )(ids, q, o, sums, delta, *[both[b] for b in blocks])


def own_kernel(q, o, sums, delta, *refs):
    both, dscores = refs[:SPAN], refs[SPAN : SPAN + 2]
    dq_hbm, part, dq, own, probs, sem = refs[SPAN + 2 :]
    key_at = lax.broadcasted_iota(jnp.int32, (TOK, TOK), 0)
    causal = key_at <= lax.broadcasted_iota(jnp.int32, (TOK, TOK), 1)
    copies = []
    for g in range(2):
        grad_tiles(g, both[:1], None, causal, q, o, sums, delta, own, (part,), probs)
        cols = slice(g * HALF, (g + 1) * HALF)
        kt = jnp.concatenate([b[:, g * HD : (g + 1) * HD].T for b in both], 1)
        d = jnp.concatenate([r[:, cols] for r in (own, *dscores)], 0)
        dqt = (dot_nn(kt, d) * SCALE).astype(BF16)
        for j in range(GROUP):
            at = g * HALF + j * HD
            dq[:, at : at + HD] = dqt[:, j * TOK : (j + 1) * TOK].T
        copies.append(pltpu.make_async_copy(dq.at[:, cols], dq_hbm.at[:, cols], sem.at[g]))
        copies[-1].start()
    for c in copies:
        c.wait()


def own(q, o, sums, delta, both, dscores):
    return pl.pallas_call(
        own_kernel,
        out_shape=[SHAPE(q.shape, BF16), SHAPE((TOK, 4 * HD), F32)],
        in_specs=[VMEM] * (4 + SPAN + 2),
        out_specs=[HBM, VMEM],
        scratch_shapes=[
            pltpu.VMEM((TOK, WIDTH), BF16),
            pltpu.VMEM((TOK, WIDTH), BF16),
            pltpu.VMEM((TOK, HALF), BF16),
            pltpu.SemaphoreType.DMA((2,)),
        ],
        **settings("own", 2, 4, 12),
    )(*in_vmem(q, o, sums, delta, *both, *dscores))


def shifted(block, by):
    devices = range(lax.axis_size("ctx"))
    return lax.ppermute(block, "ctx", [(i, i + by) for i in devices if i + by in devices])


def per_device(queries, out_grads, log_sums, deltas, keys, values, doc_ids):
    both = [join(keys, values)]
    both += [shifted(both[0], by) for by in range(1, SPAN)]
    q, o, sums, delta = load(queries[0], out_grads[0], log_sums[0], deltas[0])
    far, *parts = behind("early", EARLY, doc_ids, q, o, sums, delta, both)
    farther, *others = behind("late", LATE, doc_ids, q, o, sums, delta, both)
    parts = dict(zip(EARLY + LATE, parts + others))
    ordered = [both[b] for b in (0, *EARLY, *LATE)]
    query_grad, total = own(q, o, sums, delta, ordered, (far, farther))
    for by in range(1, SPAN):
        total = total + shifted(parts[by], -by).astype(F32)
    peers = lax.axis_size("rec")
    pieces = total.astype(BF16).reshape(peers, TOK // peers, -1)
    arrived = lax.all_to_all(pieces, "rec", 0, 0, tiled=True)
    summed = arrived.astype(F32).sum(axis=0).astype(BF16)
    return query_grad[None], summed[:, : 2 * HD], summed[:, 2 * HD :]


def solution(mesh):
    return jax.shard_map(
        per_device,
        mesh=mesh,
        in_specs=(
            P("rec", "ctx", None),
            P("rec", "ctx", None),
            P("rec", None, "ctx"),
            P("rec", None, "ctx"),
            P("ctx", None),
            P("ctx", None),
            P("rec", None),
        ),
        out_specs=(P("rec", "ctx", None), P(("ctx", "rec"), None), P(("ctx", "rec"), None)),
        check_vma=False,
    )
```

```python
import functools
import math

import jax
import jax.numpy as jnp
from jax import lax
from jax.experimental import pallas as pl
from jax.experimental.pallas import tpu as pltpu
from jax.sharding import PartitionSpec as P

HD = 128
TOK = 128
SPAN = 4
HEADS = 32
GROUP = 16
CHUNK = 2
WIDTH = HEADS * HD
HALF = GROUP * HD
SCALE = HD**-0.5
LOG2E = math.log2(math.e)
FAR = 1e30
BF16 = jnp.bfloat16
F32 = jnp.float32
EARLY, LATE = (3,), (2, 1)

VMEM = pl.BlockSpec(memory_space=pltpu.VMEM)
HBM = pl.BlockSpec(memory_space=pltpu.HBM)
SMEM = pl.BlockSpec(memory_space=pltpu.SMEM)
SHAPE = jax.ShapeDtypeStruct
PART = SHAPE((TOK, 4 * HD), BF16)


def in_hbm(*arrays):
    return [pltpu.with_memory_space_constraint(a, pltpu.HBM) for a in arrays]


def in_vmem(*arrays):
    return [pltpu.with_memory_space_constraint(a, pltpu.VMEM) for a in arrays]


def settings(name, blocks, dots, mib):
    return dict(
        name=name,
        compiler_params=pltpu.CompilerParams(vmem_limit_bytes=mib << 20),
        cost_estimate=pl.CostEstimate(
            flops=2 * dots * blocks * HEADS * TOK * TOK * HD,
            bytes_accessed=2 << 20,
            transcendentals=blocks * HEADS * TOK * TOK,
        ),
    )


def dot_nt(a, b):
    return lax.dot_general(a, b, (((1,), (1,)), ((), ())), preferred_element_type=F32)


def dot_nn(a, b):
    return lax.dot_general(a, b, (((1,), (0,)), ((), ())), preferred_element_type=F32)


def join_kernel(k, v, both, sem):
    copies = [
        pltpu.make_async_copy(k, both.at[:, : 2 * HD], sem.at[0]),
        pltpu.make_async_copy(v, both.at[:, 2 * HD :], sem.at[1]),
    ]
    for c in copies:
        c.start()
    for c in copies:
        c.wait()


def join(k, v):
    return pl.pallas_call(
        join_kernel,
        out_shape=PART,
        in_specs=[HBM, HBM],
        out_specs=VMEM,
        scratch_shapes=[pltpu.SemaphoreType.DMA((2,))],
        **settings("join", 0, 0, 1),
    )(*in_hbm(k, v))


def head_rows(ref, head, count):
    return jnp.concatenate([ref[:, h * HD : (h + 1) * HD] for h in range(head, head + count)], 0)


def grad_tiles(g, both, away, causal, q_ref, o_ref, sums_ref, delta_ref, dscores, parts, probs):
    blocks = len(both)
    k = jnp.concatenate([b[:, g * HD : (g + 1) * HD] for b in both], 0)
    v = jnp.concatenate([b[:, (g + 2) * HD : (g + 3) * HD] for b in both], 0)

    def products(i):
        head = g * GROUP + i * CHUNK
        return dot_nt(k, head_rows(q_ref, head, CHUNK)), dot_nt(v, head_rows(o_ref, head, CHUNK))

    ahead = products(0)
    for i in range(GROUP // CHUNK):
        scores, dprobs = ahead
        if (i + 1) * CHUNK < GROUP:
            ahead = products(i + 1)
        p_cols, d_cols = [], []
        for j in range(CHUNK):
            head = g * GROUP + i * CHUNK + j
            sums = sums_ref[head : head + 1, :] * LOG2E
            delta = delta_ref[head : head + 1, :]
            p_rows, d_rows = [], []
            for b in range(blocks):
                tile = slice(b * TOK, (b + 1) * TOK), slice(j * TOK, (j + 1) * TOK)
                less = sums if away is None else sums + away[b]
                p = jnp.exp2(scores[tile] * (SCALE * LOG2E) - less)
                if causal is not None:
                    p = jnp.where(causal, p, 0.0)
                p_rows.append(p.astype(BF16))
                d_rows.append((p * (dprobs[tile] - delta)).astype(BF16))
            p_cols.append(jnp.concatenate(p_rows, 0))
            d_cols.append(jnp.concatenate(d_rows, 0))
        at = i * CHUNK * TOK
        probs[:, at : at + CHUNK * TOK] = jnp.concatenate(p_cols, 1)
        at += g * HALF
        dscores[:, at : at + CHUNK * TOK] = jnp.concatenate(d_cols, 1)
    value_grad = dot_nn(probs[...], head_rows(o_ref, g * GROUP, GROUP))
    key_grad = dot_nn(dscores[:, g * HALF : (g + 1) * HALF], head_rows(q_ref, g * GROUP, GROUP))
    for b, part in enumerate(parts):
        rows = slice(b * TOK, (b + 1) * TOK)
        part[:, g * HD : (g + 1) * HD] = (key_grad[rows] * SCALE).astype(part.dtype)
        part[:, (g + 2) * HD : (g + 3) * HD] = value_grad[rows].astype(part.dtype)


def in_document(ids, back):
    me = lax.axis_index("ctx")
    at = jnp.maximum(me - back, 0)
    return jnp.logical_and(me >= back, ids[0, at] == ids[0, me])


def load_kernel(*refs):
    n = len(refs) // 2
    copies = [pltpu.make_async_copy(refs[i], refs[n + i], refs[-1].at[i]) for i in range(n)]
    for c in copies:
        c.start()
    for c in copies:
        c.wait()


def load(*arrays):
    n = len(arrays)
    return pl.pallas_call(
        load_kernel,
        out_shape=[SHAPE(a.shape, a.dtype) for a in arrays],
        in_specs=[HBM] * n,
        out_specs=[VMEM] * n,
        scratch_shapes=[pltpu.SemaphoreType.DMA((n,))],
        **settings("load", 1, 1, 2),
    )(*in_hbm(*arrays))


def behind_kernel(blocks, ids, q, o, sums, delta, *refs):
    n = len(blocks)
    both, dscores, parts, probs = refs[:n], refs[n], refs[n + 1 : -1], refs[-1]
    live = [in_document(ids, back) for back in blocks]
    away = [jnp.where(a, F32(0.0), F32(FAR)) for a in live]
    nearest = live[blocks.index(min(blocks))]

    @pl.when(nearest)
    def _():
        for g in range(2):
            grad_tiles(g, both, away, None, q, o, sums, delta, dscores, parts, probs)

    @pl.when(jnp.logical_not(nearest))
    def _():
        for ref in (dscores, *parts):
            ref[...] = jnp.zeros_like(ref)


def behind(name, blocks, ids, q, o, sums, delta, both):
    n = len(blocks)
    return pl.pallas_call(
        functools.partial(behind_kernel, blocks),
        out_shape=[SHAPE((n * TOK, WIDTH), BF16)] + [PART] * n,
        in_specs=[SMEM] + [VMEM] * (4 + n),
        out_specs=[VMEM] * (1 + n),
        scratch_shapes=[pltpu.VMEM((n * TOK, HALF), BF16)],
        **settings(name, n, 4, 12),
    )(ids, q, o, sums, delta, *[both[b] for b in blocks])


def own_kernel(q, o, sums, delta, *refs):
    both, dscores = refs[:SPAN], refs[SPAN : SPAN + 2]
    dq_hbm, part, dq, own, probs, sem = refs[SPAN + 2 :]
    key_at = lax.broadcasted_iota(jnp.int32, (TOK, TOK), 0)
    causal = key_at <= lax.broadcasted_iota(jnp.int32, (TOK, TOK), 1)
    copies = []
    for g in range(2):
        grad_tiles(g, both[:1], None, causal, q, o, sums, delta, own, (part,), probs)
        cols = slice(g * HALF, (g + 1) * HALF)
        kt = jnp.concatenate([b[:, g * HD : (g + 1) * HD].T for b in both], 1)
        d = jnp.concatenate([r[:, cols] for r in (own, *dscores)], 0)
        dqt = (dot_nn(kt, d) * SCALE).astype(BF16)
        for j in range(GROUP):
            at = g * HALF + j * HD
            dq[:, at : at + HD] = dqt[:, j * TOK : (j + 1) * TOK].T
        copies.append(pltpu.make_async_copy(dq.at[:, cols], dq_hbm.at[:, cols], sem.at[g]))
        copies[-1].start()
    for c in copies:
        c.wait()


def own(q, o, sums, delta, both, dscores):
    return pl.pallas_call(
        own_kernel,
        out_shape=[SHAPE(q.shape, BF16), SHAPE((TOK, 4 * HD), F32)],
        in_specs=[VMEM] * (4 + SPAN + 2),
        out_specs=[HBM, VMEM],
        scratch_shapes=[
            pltpu.VMEM((TOK, WIDTH), BF16),
            pltpu.VMEM((TOK, WIDTH), BF16),
            pltpu.VMEM((TOK, HALF), BF16),
            pltpu.SemaphoreType.DMA((2,)),
        ],
        **settings("own", 2, 4, 12),
    )(*in_vmem(q, o, sums, delta, *both, *dscores))


def shifted(block, by):
    devices = range(lax.axis_size("ctx"))
    return lax.ppermute(block, "ctx", [(i, i + by) for i in devices if i + by in devices])


def per_device(queries, out_grads, log_sums, deltas, keys, values, doc_ids):
    both = [join(keys, values)]
    both += [shifted(both[0], by) for by in range(1, SPAN)]
    q, o, sums, delta = load(queries[0], out_grads[0], log_sums[0], deltas[0])
    far, *parts = behind("early", EARLY, doc_ids, q, o, sums, delta, both)
    farther, *others = behind("late", LATE, doc_ids, q, o, sums, delta, both)
    parts = dict(zip(EARLY + LATE, parts + others))
    ordered = [both[b] for b in (0, *EARLY, *LATE)]
    query_grad, total = own(q, o, sums, delta, ordered, (far, farther))
    for by in range(1, SPAN):
        total = total + shifted(parts[by], -by).astype(F32)
    peers = lax.axis_size("rec")
    pieces = total.astype(BF16).reshape(peers, TOK // peers, -1)
    arrived = lax.all_to_all(pieces, "rec", 0, 0, tiled=True)
    summed = arrived.astype(F32).sum(axis=0).astype(BF16)
    return query_grad[None], summed[:, : 2 * HD], summed[:, 2 * HD :]


def solution(mesh):
    return jax.shard_map(
        per_device,
        mesh=mesh,
        in_specs=(
            P("rec", "ctx", None),
            P("rec", "ctx", None),
            P("rec", None, "ctx"),
            P("rec", None, "ctx"),
            P("ctx", None),
            P("ctx", None),
            P("rec", None),
        ),
        out_specs=(P("rec", "ctx", None), P(("ctx", "rec"), None), P(("ctx", "rec"), None)),
        check_vma=False,
    )
```

```python
import functools
import math

import jax
import jax.numpy as jnp
from jax import lax
from jax.experimental import pallas as pl
from jax.experimental.pallas import tpu as pltpu
from jax.sharding import PartitionSpec as P

HD = 128
TOK = 128
SPAN = 4
HEADS = 32
GROUP = 16
CHUNK = 2
WIDTH = HEADS * HD
HALF = GROUP * HD
SCALE = HD**-0.5
LOG2E = math.log2(math.e)
FAR = 1e30
BF16 = jnp.bfloat16
F32 = jnp.float32
EARLY, LATE = (3,), (2, 1)

VMEM = pl.BlockSpec(memory_space=pltpu.VMEM)
HBM = pl.BlockSpec(memory_space=pltpu.HBM)
SMEM = pl.BlockSpec(memory_space=pltpu.SMEM)
SHAPE = jax.ShapeDtypeStruct
PART = SHAPE((TOK, 4 * HD), BF16)


def in_hbm(*arrays):
    return [pltpu.with_memory_space_constraint(a, pltpu.HBM) for a in arrays]


def in_vmem(*arrays):
    return [pltpu.with_memory_space_constraint(a, pltpu.VMEM) for a in arrays]


def settings(name, blocks, dots, mib):
    return dict(
        name=name,
        compiler_params=pltpu.CompilerParams(vmem_limit_bytes=mib << 20),
        cost_estimate=pl.CostEstimate(
            flops=2 * dots * blocks * HEADS * TOK * TOK * HD,
            bytes_accessed=2 << 20,
            transcendentals=blocks * HEADS * TOK * TOK,
        ),
    )


def dot_nt(a, b):
    return lax.dot_general(a, b, (((1,), (1,)), ((), ())), preferred_element_type=F32)


def dot_nn(a, b):
    return lax.dot_general(a, b, (((1,), (0,)), ((), ())), preferred_element_type=F32)


def join_kernel(k, v, both, sem):
    copies = [
        pltpu.make_async_copy(k, both.at[:, : 2 * HD], sem.at[0]),
        pltpu.make_async_copy(v, both.at[:, 2 * HD :], sem.at[1]),
    ]
    for c in copies:
        c.start()
    for c in copies:
        c.wait()


def join(k, v):
    return pl.pallas_call(
        join_kernel,
        out_shape=PART,
        in_specs=[HBM, HBM],
        out_specs=VMEM,
        scratch_shapes=[pltpu.SemaphoreType.DMA((2,))],
        **settings("join", 0, 0, 1),
    )(*in_hbm(k, v))


def head_rows(ref, head, count):
    return jnp.concatenate([ref[:, h * HD : (h + 1) * HD] for h in range(head, head + count)], 0)


def grad_tiles(g, both, away, causal, q_ref, o_ref, sums_ref, delta_ref, dscores, parts, probs):
    blocks = len(both)
    k = jnp.concatenate([b[:, g * HD : (g + 1) * HD] for b in both], 0)
    v = jnp.concatenate([b[:, (g + 2) * HD : (g + 3) * HD] for b in both], 0)

    def products(i):
        head = g * GROUP + i * CHUNK
        return dot_nt(k, head_rows(q_ref, head, CHUNK)), dot_nt(v, head_rows(o_ref, head, CHUNK))

    ahead = products(0)
    for i in range(GROUP // CHUNK):
        scores, dprobs = ahead
        if (i + 1) * CHUNK < GROUP:
            ahead = products(i + 1)
        p_cols, d_cols = [], []
        for j in range(CHUNK):
            head = g * GROUP + i * CHUNK + j
            sums = sums_ref[head : head + 1, :] * LOG2E
            delta = delta_ref[head : head + 1, :]
            p_rows, d_rows = [], []
            for b in range(blocks):
                tile = slice(b * TOK, (b + 1) * TOK), slice(j * TOK, (j + 1) * TOK)
                less = sums if away is None else sums + away[b]
                p = jnp.exp2(scores[tile] * (SCALE * LOG2E) - less)
                if causal is not None:
                    p = jnp.where(causal, p, 0.0)
                p_rows.append(p.astype(BF16))
                d_rows.append((p * (dprobs[tile] - delta)).astype(BF16))
            p_cols.append(jnp.concatenate(p_rows, 0))
            d_cols.append(jnp.concatenate(d_rows, 0))
        at = i * CHUNK * TOK
        probs[:, at : at + CHUNK * TOK] = jnp.concatenate(p_cols, 1)
        at += g * HALF
        dscores[:, at : at + CHUNK * TOK] = jnp.concatenate(d_cols, 1)
    value_grad = dot_nn(probs[...], head_rows(o_ref, g * GROUP, GROUP))
    key_grad = dot_nn(dscores[:, g * HALF : (g + 1) * HALF], head_rows(q_ref, g * GROUP, GROUP))
    for b, part in enumerate(parts):
        rows = slice(b * TOK, (b + 1) * TOK)
        part[:, g * HD : (g + 1) * HD] = (key_grad[rows] * SCALE).astype(part.dtype)
        part[:, (g + 2) * HD : (g + 3) * HD] = value_grad[rows].astype(part.dtype)


def in_document(ids, back):
    me = lax.axis_index("ctx")
    at = jnp.maximum(me - back, 0)
    return jnp.logical_and(me >= back, ids[0, at] == ids[0, me])


def load_kernel(*refs):
    n = len(refs) // 2
    copies = [pltpu.make_async_copy(refs[i], refs[n + i], refs[-1].at[i]) for i in range(n)]
    for c in copies:
        c.start()
    for c in copies:
        c.wait()


def load(*arrays):
    n = len(arrays)
    return pl.pallas_call(
        load_kernel,
        out_shape=[SHAPE(a.shape, a.dtype) for a in arrays],
        in_specs=[HBM] * n,
        out_specs=[VMEM] * n,
        scratch_shapes=[pltpu.SemaphoreType.DMA((n,))],
        **settings("load", 1, 1, 2),
    )(*in_hbm(*arrays))


def behind_kernel(blocks, ids, q, o, sums, delta, *refs):
    n = len(blocks)
    both, dscores, parts, probs = refs[:n], refs[n], refs[n + 1 : -1], refs[-1]
    live = [in_document(ids, back) for back in blocks]
    away = [jnp.where(a, F32(0.0), F32(FAR)) for a in live]
    for dead in range(n + 1):
        rows = pl.ds(dead * TOK, (n - dead) * TOK)
        here = True if dead == n else live[dead]
        if dead:
            here = jnp.logical_and(here, jnp.logical_not(live[dead - 1]))

        @pl.when(here)
        def _():
            if dead:
                dscores[: dead * TOK] = jnp.zeros((dead * TOK, WIDTH), BF16)
            for part in parts[:dead]:
                part[...] = jnp.zeros_like(part)
            for g in range(2 if dead < n else 0):
                grad_tiles(
                    g, both[dead:], away[dead:], None, q, o, sums, delta,
                    dscores.at[rows], parts[dead:], probs.at[rows],
                )


def behind(name, blocks, ids, q, o, sums, delta, both):
    n = len(blocks)
    return pl.pallas_call(
        functools.partial(behind_kernel, blocks),
        out_shape=[SHAPE((n * TOK, WIDTH), BF16)] + [PART] * n,
        in_specs=[SMEM] + [VMEM] * (4 + n),
        out_specs=[VMEM] * (1 + n),
        scratch_shapes=[pltpu.VMEM((n * TOK, HALF), BF16)],
        **settings(name, n, 4, 12),
    )(ids, q, o, sums, delta, *[both[b] for b in blocks])


def own_kernel(q, o, sums, delta, *refs):
    both, dscores = refs[:SPAN], refs[SPAN : SPAN + 2]
    dq_hbm, part, dq, own, probs, sem = refs[SPAN + 2 :]
    key_at = lax.broadcasted_iota(jnp.int32, (TOK, TOK), 0)
    causal = key_at <= lax.broadcasted_iota(jnp.int32, (TOK, TOK), 1)
    copies = []
    for g in range(2):
        grad_tiles(g, both[:1], None, causal, q, o, sums, delta, own, (part,), probs)
        cols = slice(g * HALF, (g + 1) * HALF)
        kt = jnp.concatenate([b[:, g * HD : (g + 1) * HD].T for b in both], 1)
        d = jnp.concatenate([r[:, cols] for r in (own, *dscores)], 0)
        dqt = (dot_nn(kt, d) * SCALE).astype(BF16)
        for j in range(GROUP):
            at = g * HALF + j * HD
            dq[:, at : at + HD] = dqt[:, j * TOK : (j + 1) * TOK].T
        copies.append(pltpu.make_async_copy(dq.at[:, cols], dq_hbm.at[:, cols], sem.at[g]))
        copies[-1].start()
    for c in copies:
        c.wait()


def own(q, o, sums, delta, both, dscores):
    return pl.pallas_call(
        own_kernel,
        out_shape=[SHAPE(q.shape, BF16), SHAPE((TOK, 4 * HD), F32)],
        in_specs=[VMEM] * (4 + SPAN + 2),
        out_specs=[HBM, VMEM],
        scratch_shapes=[
            pltpu.VMEM((TOK, WIDTH), BF16),
            pltpu.VMEM((TOK, WIDTH), BF16),
            pltpu.VMEM((TOK, HALF), BF16),
            pltpu.SemaphoreType.DMA((2,)),
        ],
        **settings("own", 2, 4, 12),
    )(*in_vmem(q, o, sums, delta, *both, *dscores))


def shifted(block, by):
    devices = range(lax.axis_size("ctx"))
    return lax.ppermute(block, "ctx", [(i, i + by) for i in devices if i + by in devices])


def per_device(queries, out_grads, log_sums, deltas, keys, values, doc_ids):
    both = [join(keys, values)]
    both += [shifted(both[0], by) for by in range(1, SPAN)]
    q, o, sums, delta = load(queries[0], out_grads[0], log_sums[0], deltas[0])
    far, *parts = behind("early", EARLY, doc_ids, q, o, sums, delta, both)
    farther, *others = behind("late", LATE, doc_ids, q, o, sums, delta, both)
    parts = dict(zip(EARLY + LATE, parts + others))
    ordered = [both[b] for b in (0, *EARLY, *LATE)]
    query_grad, total = own(q, o, sums, delta, ordered, (far, farther))
    for by in range(1, SPAN):
        total = total + shifted(parts[by], -by).astype(F32)
    peers = lax.axis_size("rec")
    pieces = total.astype(BF16).reshape(peers, TOK // peers, -1)
    arrived = lax.all_to_all(pieces, "rec", 0, 0, tiled=True)
    summed = arrived.astype(F32).sum(axis=0).astype(BF16)
    return query_grad[None], summed[:, : 2 * HD], summed[:, 2 * HD :]


def solution(mesh):
    return jax.shard_map(
        per_device,
        mesh=mesh,
        in_specs=(
            P("rec", "ctx", None),
            P("rec", "ctx", None),
            P("rec", None, "ctx"),
            P("rec", None, "ctx"),
            P("ctx", None),
            P("ctx", None),
            P("rec", None),
        ),
        out_specs=(P("rec", "ctx", None), P(("ctx", "rec"), None), P(("ctx", "rec"), None)),
        check_vma=False,
    )
```

```python
import functools
import math

import jax
import jax.numpy as jnp
from jax import lax
from jax.experimental import pallas as pl
from jax.experimental.pallas import tpu as pltpu
from jax.sharding import PartitionSpec as P

HD = 128
TOK = 128
SPAN = 4
HEADS = 32
GROUP = 16
CHUNK = 4
WIDTH = HEADS * HD
HALF = GROUP * HD
SCALE = HD**-0.5
LOG2E = math.log2(math.e)
FAR = 1e30
BF16 = jnp.bfloat16
F32 = jnp.float32
EARLY, LATE = (3,), (2, 1)

VMEM = pl.BlockSpec(memory_space=pltpu.VMEM)
HBM = pl.BlockSpec(memory_space=pltpu.HBM)
SMEM = pl.BlockSpec(memory_space=pltpu.SMEM)
SHAPE = jax.ShapeDtypeStruct
PART = SHAPE((TOK, 4 * HD), BF16)


def in_hbm(*arrays):
    return [pltpu.with_memory_space_constraint(a, pltpu.HBM) for a in arrays]


def in_vmem(*arrays):
    return [pltpu.with_memory_space_constraint(a, pltpu.VMEM) for a in arrays]


def settings(name, blocks, dots, mib):
    return dict(
        name=name,
        compiler_params=pltpu.CompilerParams(vmem_limit_bytes=mib << 20),
        cost_estimate=pl.CostEstimate(
            flops=2 * dots * blocks * HEADS * TOK * TOK * HD,
            bytes_accessed=2 << 20,
            transcendentals=blocks * HEADS * TOK * TOK,
        ),
    )


def dot_nt(a, b):
    return lax.dot_general(a, b, (((1,), (1,)), ((), ())), preferred_element_type=F32)


def dot_nn(a, b):
    return lax.dot_general(a, b, (((1,), (0,)), ((), ())), preferred_element_type=F32)


def join_kernel(k, v, both, sem):
    copies = [
        pltpu.make_async_copy(k, both.at[:, : 2 * HD], sem.at[0]),
        pltpu.make_async_copy(v, both.at[:, 2 * HD :], sem.at[1]),
    ]
    for c in copies:
        c.start()
    for c in copies:
        c.wait()


def join(k, v):
    return pl.pallas_call(
        join_kernel,
        out_shape=PART,
        in_specs=[HBM, HBM],
        out_specs=VMEM,
        scratch_shapes=[pltpu.SemaphoreType.DMA((2,))],
        **settings("join", 0, 0, 1),
    )(*in_hbm(k, v))


def head_rows(ref, head, count):
    return jnp.concatenate([ref[:, h * HD : (h + 1) * HD] for h in range(head, head + count)], 0)


def grad_tiles(g, both, away, causal, q_ref, o_ref, sums_ref, delta_ref, dscores, parts, probs):
    blocks = len(both)
    k = jnp.concatenate([b[:, g * HD : (g + 1) * HD] for b in both], 0)
    v = jnp.concatenate([b[:, (g + 2) * HD : (g + 3) * HD] for b in both], 0)

    def products(i):
        head = g * GROUP + i * CHUNK
        return dot_nt(k, head_rows(q_ref, head, CHUNK)), dot_nt(v, head_rows(o_ref, head, CHUNK))

    ahead = products(0)
    for i in range(GROUP // CHUNK):
        scores, dprobs = ahead
        if (i + 1) * CHUNK < GROUP:
            ahead = products(i + 1)
        p_cols, d_cols = [], []
        for j in range(CHUNK):
            head = g * GROUP + i * CHUNK + j
            sums = sums_ref[head : head + 1, :] * LOG2E
            delta = delta_ref[head : head + 1, :]
            p_rows, d_rows = [], []
            for b in range(blocks):
                tile = slice(b * TOK, (b + 1) * TOK), slice(j * TOK, (j + 1) * TOK)
                less = sums if away is None else sums + away[b]
                p = jnp.exp2(scores[tile] * (SCALE * LOG2E) - less)
                if causal is not None:
                    p = jnp.where(causal, p, 0.0)
                p_rows.append(p.astype(BF16))
                d_rows.append((p * (dprobs[tile] - delta)).astype(BF16))
            p_cols.append(jnp.concatenate(p_rows, 0))
            d_cols.append(jnp.concatenate(d_rows, 0))
        at = i * CHUNK * TOK
        probs[:, at : at + CHUNK * TOK] = jnp.concatenate(p_cols, 1)
        at += g * HALF
        dscores[:, at : at + CHUNK * TOK] = jnp.concatenate(d_cols, 1)
    value_grad = dot_nn(probs[...], head_rows(o_ref, g * GROUP, GROUP))
    key_grad = dot_nn(dscores[:, g * HALF : (g + 1) * HALF], head_rows(q_ref, g * GROUP, GROUP))
    for b, part in enumerate(parts):
        rows = slice(b * TOK, (b + 1) * TOK)
        part[:, g * HD : (g + 1) * HD] = (key_grad[rows] * SCALE).astype(part.dtype)
        part[:, (g + 2) * HD : (g + 3) * HD] = value_grad[rows].astype(part.dtype)


def in_document(ids, back):
    me = lax.axis_index("ctx")
    at = jnp.maximum(me - back, 0)
    return jnp.logical_and(me >= back, ids[0, at] == ids[0, me])


def load_kernel(*refs):
    n = len(refs) // 2
    copies = [pltpu.make_async_copy(refs[i], refs[n + i], refs[-1].at[i]) for i in range(n)]
    for c in copies:
        c.start()
    for c in copies:
        c.wait()


def load(*arrays):
    n = len(arrays)
    return pl.pallas_call(
        load_kernel,
        out_shape=[SHAPE(a.shape, a.dtype) for a in arrays],
        in_specs=[HBM] * n,
        out_specs=[VMEM] * n,
        scratch_shapes=[pltpu.SemaphoreType.DMA((n,))],
        **settings("load", 1, 1, 2),
    )(*in_hbm(*arrays))


def behind_kernel(blocks, ids, q, o, sums, delta, *refs):
    n = len(blocks)
    both, dscores, parts, probs = refs[:n], refs[n], refs[n + 1 : -1], refs[-1]
    live = [in_document(ids, back) for back in blocks]
    away = [jnp.where(a, F32(0.0), F32(FAR)) for a in live]
    for dead in range(n + 1):
        rows = pl.ds(dead * TOK, (n - dead) * TOK)
        here = True if dead == n else live[dead]
        if dead:
            here = jnp.logical_and(here, jnp.logical_not(live[dead - 1]))

        @pl.when(here)
        def _():
            if dead:
                dscores[: dead * TOK] = jnp.zeros((dead * TOK, WIDTH), BF16)
            for part in parts[:dead]:
                part[...] = jnp.zeros_like(part)
            for g in range(2 if dead < n else 0):
                grad_tiles(
                    g, both[dead:], away[dead:], None, q, o, sums, delta,
                    dscores.at[rows], parts[dead:], probs.at[rows],
                )


def behind(name, blocks, ids, q, o, sums, delta, both):
    n = len(blocks)
    return pl.pallas_call(
        functools.partial(behind_kernel, blocks),
        out_shape=[SHAPE((n * TOK, WIDTH), BF16)] + [PART] * n,
        in_specs=[SMEM] + [VMEM] * (4 + n),
        out_specs=[VMEM] * (1 + n),
        scratch_shapes=[pltpu.VMEM((n * TOK, HALF), BF16)],
        **settings(name, n, 4, 12),
    )(ids, q, o, sums, delta, *[both[b] for b in blocks])


def own_kernel(q, o, sums, delta, *refs):
    both, dscores = refs[:SPAN], refs[SPAN : SPAN + 2]
    dq_hbm, part, dq, own, probs, sem = refs[SPAN + 2 :]
    key_at = lax.broadcasted_iota(jnp.int32, (TOK, TOK), 0)
    causal = key_at <= lax.broadcasted_iota(jnp.int32, (TOK, TOK), 1)
    copies = []
    for g in range(2):
        grad_tiles(g, both[:1], None, causal, q, o, sums, delta, own, (part,), probs)
        cols = slice(g * HALF, (g + 1) * HALF)
        kt = jnp.concatenate([b[:, g * HD : (g + 1) * HD].T for b in both], 1)
        d = jnp.concatenate([r[:, cols] for r in (own, *dscores)], 0)
        dqt = (dot_nn(kt, d) * SCALE).astype(BF16)
        for j in range(GROUP):
            at = g * HALF + j * HD
            dq[:, at : at + HD] = dqt[:, j * TOK : (j + 1) * TOK].T
        copies.append(pltpu.make_async_copy(dq.at[:, cols], dq_hbm.at[:, cols], sem.at[g]))
        copies[-1].start()
    for c in copies:
        c.wait()


def own(q, o, sums, delta, both, dscores):
    return pl.pallas_call(
        own_kernel,
        out_shape=[SHAPE(q.shape, BF16), SHAPE((TOK, 4 * HD), F32)],
        in_specs=[VMEM] * (4 + SPAN + 2),
        out_specs=[HBM, VMEM],
        scratch_shapes=[
            pltpu.VMEM((TOK, WIDTH), BF16),
            pltpu.VMEM((TOK, WIDTH), BF16),
            pltpu.VMEM((TOK, HALF), BF16),
            pltpu.SemaphoreType.DMA((2,)),
        ],
        **settings("own", 2, 4, 12),
    )(*in_vmem(q, o, sums, delta, *both, *dscores))


def shifted(block, by):
    devices = range(lax.axis_size("ctx"))
    return lax.ppermute(block, "ctx", [(i, i + by) for i in devices if i + by in devices])


def per_device(queries, out_grads, log_sums, deltas, keys, values, doc_ids):
    both = [join(keys, values)]
    both += [shifted(both[0], by) for by in range(1, SPAN)]
    q, o, sums, delta = load(queries[0], out_grads[0], log_sums[0], deltas[0])
    far, *parts = behind("early", EARLY, doc_ids, q, o, sums, delta, both)
    farther, *others = behind("late", LATE, doc_ids, q, o, sums, delta, both)
    parts = dict(zip(EARLY + LATE, parts + others))
    ordered = [both[b] for b in (0, *EARLY, *LATE)]
    query_grad, total = own(q, o, sums, delta, ordered, (far, farther))
    for by in range(1, SPAN):
        total = total + shifted(parts[by], -by).astype(F32)
    peers = lax.axis_size("rec")
    pieces = total.astype(BF16).reshape(peers, TOK // peers, -1)
    arrived = lax.all_to_all(pieces, "rec", 0, 0, tiled=True)
    summed = arrived.astype(F32).sum(axis=0).astype(BF16)
    return query_grad[None], summed[:, : 2 * HD], summed[:, 2 * HD :]


def solution(mesh):
    return jax.shard_map(
        per_device,
        mesh=mesh,
        in_specs=(
            P("rec", "ctx", None),
            P("rec", "ctx", None),
            P("rec", None, "ctx"),
            P("rec", None, "ctx"),
            P("ctx", None),
            P("ctx", None),
            P("rec", None),
        ),
        out_specs=(P("rec", "ctx", None), P(("ctx", "rec"), None), P(("ctx", "rec"), None)),
        check_vma=False,
    )
```
